256 devices in a mesh: fsdp: 64 (over x_hi, z, y), grp: 4 (over x_lo, core).
Axes of the slice: x: 4 (x_hi: 2, x_lo: 2; x = x_hi * 2 + x_lo), y: 4, z: 8, core: 2. Of those that a mesh axis runs over, the one named last changes fastest.
Arguments:
- weight: bfloat16 [26624, 8192], P('fsdp', 'grp'), may hold values from -6 to 6
Outputs:
- quantized: bfloat16 [26624, 8192], P('grp', 'fsdp')
- scales: float32 [208, 64], P('grp', 'fsdp')
The draws below stay inside these ranges and needn't reach their ends.
All inputs are finite; a program needn't handle non-finite values. Where the reference program divides by a largest or mean magnitude, that divisor is 1e-20 or more.
Results may differ from the reference program's by a relative error of at most 0.001.
Values sent between devices are 32-bit elements; how exact they have to be, the bound alone decides.
A program may use at most 128 MiB of HBM per device.

```python
import math
import jax
import jax.numpy as jnp
import numpy as np
from jax import lax

D = 8192
HB = 512
BLOCK = 128
FF = 26624
N_FSDP = 64
N_GRP = 4


def steps_of(rng, extent, shards, low, top_value):
    def one(axis_at, blocks):
        draws = jax.random.uniform(jax.random.fold_in(jax.random.fold_in(rng, 6), axis_at), (blocks,), jnp.float32, low / len(shards), top_value / len(shards))
        return jnp.repeat(jnp.exp(draws), extent[axis_at] // blocks).reshape((-1,) + (1,) * (len(extent) - axis_at - 1))

    factor_of = one(*shards[0])
    for cut in shards[1:]:
        factor_of = factor_of * one(*cut)
    return factor_of


def noise(rng, extent, scale, bound, split=(), kind=jnp.bfloat16):
    values = scale * jax.random.normal(rng, extent, jnp.float32)
    if split:
        values = values * steps_of(rng, extent, split, -0.22, 0.18)
    return jnp.clip(values, -bound, bound).astype(kind)


def setup_inputs(seed: int = 0) -> dict:
    key_list = jax.random.split(jax.random.key(seed), 2)
    return {
        "weight": noise(key_list[0], (FF, D), 1.0, 6.0, ((0, 64), (1, 4))),
    }


def paley_signs():
    squares_set = set()
    for coord_one in range(5):
        for coord_two in range(5):
            if coord_one or coord_two:
                squares_set.add(((coord_one * coord_one + 2 * coord_two * coord_two) % 5, 2 * coord_one * coord_two % 5))
    conference = np.zeros((26, 26), np.float32)
    conference[0, 1:] = 1.0
    conference[1:, 0] = 1.0
    for row_elem in range(25):
        for col_elem in range(25):
            diff_one = (row_elem % 5 - col_elem % 5) % 5
            diff_two = (row_elem // 5 - col_elem // 5) % 5
            if diff_one or diff_two:
                conference[1 + row_elem, 1 + col_elem] = 1.0 if (diff_one, diff_two) in squares_set else -1.0
    plus_block = np.array([[1.0, 1.0], [1.0, -1.0]], np.float32)
    minus_block = np.array([[1.0, -1.0], [-1.0, -1.0]], np.float32)
    return (np.kron(conference, plus_block) + np.kron(np.eye(26, dtype=np.float32), minus_block)).astype(np.float32)

def sylvester(order):
    indices = jnp.arange(order, dtype=jnp.int32)
    parity = jnp.zeros((order, order), jnp.int32)
    for bit_pos in range(max(order.bit_length() - 1, 0)):
        parity = parity + (indices[:, None] >> bit_pos & 1) * (indices[None, :] >> bit_pos & 1)
    return (1 - 2 * (parity % 2)).astype(jnp.float32)

def apply_axis(values, matrix, axis_pos):
    product = jnp.tensordot(matrix, values, axes=([1], [axis_pos]), precision=lax.Precision.HIGHEST)
    return jnp.moveaxis(product, 0, axis_pos)

def apply_sylvester(values, order, axis_pos):
    inner_order = min(order, 32)
    outer_order = order // inner_order
    dims_now = values.shape
    values = values.reshape(dims_now[:axis_pos] + (outer_order, inner_order) + dims_now[axis_pos + 1:])
    values = apply_axis(values, sylvester(outer_order), axis_pos)
    values = apply_axis(values, sylvester(inner_order), axis_pos + 1)
    return values.reshape(dims_now)

def reference(weight):
    values = weight.astype(jnp.float32).reshape(HB, 52, D)
    values = apply_axis(values, jnp.asarray(paley_signs(), jnp.float32), 1)
    values = apply_sylvester(values, HB, 0)
    values = values.reshape(HB, 52, N_GRP, D // N_GRP)
    values = apply_axis(values, sylvester(N_GRP), 2)
    values = apply_sylvester(values, D // N_GRP, 3)
    values = values.reshape(HB, 52, N_GRP, N_FSDP, D // (N_GRP * N_FSDP))
    values = values.transpose(0, 1, 3, 2, 4).reshape(FF, D)
    values = values * (1.0 / math.sqrt(FF * D))
    blocks = values.reshape(FF // BLOCK, BLOCK, D // BLOCK, BLOCK)
    scales = lax.optimization_barrier(jnp.max(jnp.abs(blocks), axis=(1, 3)))
    quantized = (blocks / (scales[:, None, :, None] + 1e-06)).astype(jnp.bfloat16).reshape(FF, D)
    return (quantized, scales)
```

```python
import functools
import math

import jax
import jax.numpy as jnp
import numpy as np
from jax import lax
from jax.experimental import pallas as pl
from jax.experimental.pallas import tpu as pltpu
from jax.sharding import PartitionSpec as P

MESH = pl.DeviceIdType.MESH
D = 8192
BLOCK = 128
FF = 26624
N_F = 64
N_G = 4
ROWS = FF // N_F
COLS = D // N_G
SUB = ROWS // 4
COEF = 1.0 / math.sqrt(FF * D)
CHUNKS = ((0, 32), (32, 32), (64, 24), (88, 16))


def paley_signs():
    squares_set = set()
    for coord_one in range(5):
        for coord_two in range(5):
            if coord_one or coord_two:
                squares_set.add(
                    (
                        (coord_one * coord_one + 2 * coord_two * coord_two) % 5,
                        2 * coord_one * coord_two % 5,
                    )
                )
    conference = np.zeros((26, 26), np.float32)
    conference[0, 1:] = 1.0
    conference[1:, 0] = 1.0
    for row_elem in range(25):
        for col_elem in range(25):
            diff_one = (row_elem % 5 - col_elem % 5) % 5
            diff_two = (row_elem // 5 - col_elem // 5) % 5
            if diff_one or diff_two:
                conference[1 + row_elem, 1 + col_elem] = (
                    1.0 if (diff_one, diff_two) in squares_set else -1.0
                )
    plus_block = np.array([[1.0, 1.0], [1.0, -1.0]], np.float32)
    minus_block = np.array([[1.0, -1.0], [-1.0, -1.0]], np.float32)
    return np.kron(conference, plus_block) + np.kron(np.eye(26), minus_block)


def sylvester(order):
    signs = np.ones((1, 1), np.float32)
    while signs.shape[0] < order:
        signs = np.kron(np.array([[1.0, 1.0], [1.0, -1.0]]), signs)
    return signs


def butterflies(values):
    values = list(values)
    step = 1
    while step < len(values):
        for i in range(len(values)):
            if not i & step:
                a, b = values[i], values[i | step]
                values[i], values[i | step] = a + b, a - b
        step *= 2
    return values


def block_transpose(h, low_half, even_block):
    out = list(h)
    for a in (0, 1):
        t = pltpu.roll(jnp.where(low_half, h[a + 2], h[a]), 64, 1)
        out[a] = jnp.where(low_half, h[a], t)
        out[a + 2] = jnp.where(low_half, t, h[a + 2])
    h, out = out, list(out)
    for a in (0, 2):
        out[a] = jnp.where(even_block, h[a], pltpu.roll(h[a + 1], 32, 1))
        out[a + 1] = jnp.where(even_block, pltpu.roll(h[a], 96, 1), h[a + 1])
    return out


def kernel(
    w_hbm, l_hbm, s_hbm, q_hbm, scale_ref,
    w, l, s256, x, s1, r1, z, g, o, m8, inv, qv,
    load_sem, send1, recv1, send2, recv2, out_sem,
):
    me_f, me_g = lax.axis_index("fsdp"), lax.axis_index("grp")
    loads = [
        pltpu.make_async_copy(src, dst, load_sem.at[i])
        for i, (src, dst) in enumerate(((w_hbm, w), (l_hbm, l), (s_hbm, s256)))
    ]
    for copy in loads:
        copy.start()

    def peer(i):
        k, rest = i % 8, i // 8
        odd = k % 2
        dz = odd * ((k + 1) // 2) + (1 - odd) * (8 - k // 2)
        dx, dy = rest // 4, rest % 4
        px = (me_f // 32 + dx) % 2
        pz = ((me_f // 4) % 8 + dz) % 8
        py = (me_f % 4 + dy) % 4
        return px * 32 + pz * 4 + py

    barrier = pltpu.get_barrier_semaphore()

    @pl.loop(1, N_F)
    def _(i):
        pl.semaphore_signal(barrier, inc=1, device_id=(peer(i), me_g), device_id_type=MESH)

    @pl.loop(1, N_G)
    def _(i):
        pl.semaphore_signal(barrier, inc=1, device_id=(me_f, (me_g + i) % N_G), device_id_type=MESH)

    lane = lax.broadcasted_iota(jnp.int32, (8, 128), 1)
    low_half = lane < 64
    even_block = (lane // 32) % 2 == 0
    m8[...] = jnp.zeros_like(m8)
    for copy in loads:
        copy.wait()

    def local_part(r0, n):
        lhs = l[4 * r0 : 4 * (r0 + n), :]
        for u in range(8):
            cols = slice(256 * u, 256 * (u + 1))
            part = jnp.dot(lhs, w[:, cols], preferred_element_type=jnp.float32)
            hi = part.astype(jnp.bfloat16)
            lo = (part - hi.astype(jnp.float32)).astype(jnp.bfloat16)
            x[u, : 4 * n, :] = jnp.dot(
                hi, s256[...], preferred_element_type=jnp.float32
            ) + jnp.dot(lo, s256[...], preferred_element_type=jnp.float32)

        @pl.loop(0, n // 8)
        def _(k):
            row = pl.multiple_of(k * 8, 8)
            for half in range(2):
                lanes = slice(128 * half, 128 * (half + 1))
                got = [
                    butterflies([x[u, pl.ds(row + a * n, 8), lanes] for u in range(8)])
                    for a in range(4)
                ]
                for u in range(8):
                    parts = block_transpose([got[a][u] for a in range(4)], low_half, even_block)
                    for b in range(4):
                        s1[(u * 2 + half) * 4 + b, pl.ds(r0 + row, 8), :] = parts[b]

    def send_fsdp(c, r0, n):
        rows = pl.ds(r0, n)
        pltpu.make_async_copy(s1.at[me_f, rows], r1.at[me_f, rows], recv1.at[c]).start()

        @pl.loop(1, N_F)
        def _(i):
            p = peer(i)
            pltpu.make_async_remote_copy(
                src_ref=s1.at[p, rows],
                dst_ref=r1.at[me_f, rows],
                send_sem=send1.at[c],
                recv_sem=recv1.at[c],
                device_id=(p, me_g),
                device_id_type=MESH,
            ).start()

    def fsdp_part(c, r0, n):
        rows = pl.ds(r0, n)
        pltpu.make_async_copy(r1.at[:, rows], r1.at[:, rows], recv1.at[c]).wait()

        @pl.loop(0, n // 8)
        def _(k):
            row = pl.ds(pl.multiple_of(r0 + k * 8, 8), 8)
            for a in range(8):
                got = butterflies([r1[a * 8 + b, row, :] for b in range(8)])
                for b in range(8):
                    z[a * 8 + b, row, :] = got[b]
            for b in range(8):
                got = butterflies([z[a * 8 + b, row, :] for a in range(8)])
                for a in range(8):
                    z[a * 8 + b, row, :] = got[a]

    def send_grp(c, r0, n):
        rows = pl.ds(r0, n)
        pltpu.make_async_copy(
            z.at[pl.ds(me_g * 16, 16), rows], g.at[me_g, :, rows], recv2.at[c]
        ).start()

        @pl.loop(1, N_G)
        def _(i):
            q = (me_g + i) % N_G
            pltpu.make_async_remote_copy(
                src_ref=z.at[pl.ds(q * 16, 16), rows],
                dst_ref=g.at[me_g, :, rows],
                send_sem=send2.at[c],
                recv_sem=recv2.at[c],
                device_id=(me_f, q),
                device_id_type=MESH,
            ).start()

    def grp_part(c, r0, n):
        rows = pl.ds(r0, n)
        pltpu.make_async_copy(g.at[:, :, rows], g.at[:, :, rows], recv2.at[c]).wait()

        @pl.loop(0, 16)
        def _(m):
            for k in range(n // 8):
                tile = r0 // 8 + k
                row = pl.ds(tile * 8, 8)
                got = butterflies([g[a, m, row, :] for a in range(4)])
                parts = block_transpose(got, low_half, even_block)
                for b in range(4):
                    at = (m * 4 + b) * (SUB // 8) + tile
                    o[pl.ds(pl.multiple_of(at * 8, 8), 8), :] = parts[b]
                    m8[at // 16] = jnp.maximum(m8[at // 16], jnp.abs(parts[b]))

    last = len(CHUNKS) - 1
    local_part(*CHUNKS[0])
    pl.semaphore_wait(barrier, N_F + N_G - 2)
    send_fsdp(0, *CHUNKS[0])
    for c in range(1, last + 1):
        local_part(*CHUNKS[c])
        send_fsdp(c, *CHUNKS[c])
    for c in range(last + 1):
        fsdp_part(c, *CHUNKS[c])
        send_grp(c, *CHUNKS[c])
        if c:
            grp_part(c - 1, *CHUNKS[c - 1])
    grp_part(last, *CHUNKS[last])

    top = jnp.max(jnp.max(m8[...], axis=1), axis=1, keepdims=True) * COEF
    scale_ref[...] = top
    inv[...] = jnp.broadcast_to(COEF / (top + 1e-06), (52, 128))
    quarter = 52 // 4
    outs = []
    for part in range(4):

        @pl.loop(part * quarter, (part + 1) * quarter)
        def _(i):
            rows = pl.ds(pl.multiple_of(i * BLOCK, BLOCK), BLOCK)
            qv[rows, :] = (o[rows, :] * inv[pl.ds(i, 1), :]).astype(jnp.bfloat16)

        rows = pl.ds(part * quarter * BLOCK, quarter * BLOCK)
        outs.append(pltpu.make_async_copy(qv.at[rows], q_hbm.at[rows], out_sem.at[part]))
        outs[-1].start()
    for copy in outs:
        copy.wait()
    for c, (r0, n) in enumerate(CHUNKS):
        sent = s1.at[pl.ds(0, N_F - 1), pl.ds(r0, n)]
        pltpu.make_async_copy(sent, sent, send1.at[c]).wait()
        sent = z.at[pl.ds(0, 48), pl.ds(r0, n)]
        pltpu.make_async_copy(sent, sent, send2.at[c]).wait()


def body(weight):
    full = np.kron(sylvester(8), paley_signs())
    order = np.concatenate(
        [a * SUB + np.arange(r0, r0 + n) for r0, n in CHUNKS for a in range(4)]
    )
    left = jnp.asarray(full[order], jnp.bfloat16)
    right = jnp.asarray(sylvester(256), jnp.bfloat16)
    count = len(CHUNKS)
    f32, bf16 = jnp.float32, jnp.bfloat16
    top_rows = 4 * max(n for _, n in CHUNKS)
    dma = pltpu.SemaphoreType.DMA
    return pl.pallas_call(
        kernel,
        out_shape=(
            jax.ShapeDtypeStruct((FF // N_G, D // N_F), bf16),
            jax.ShapeDtypeStruct((52, 1), f32),
        ),
        in_specs=[pl.BlockSpec(memory_space=pl.ANY)] * 3,
        out_specs=(
            pl.BlockSpec(memory_space=pl.ANY),
            pl.BlockSpec(memory_space=pltpu.VMEM),
        ),
        scratch_shapes=[
            pltpu.VMEM((ROWS, COLS), bf16),
            pltpu.VMEM((ROWS, ROWS), bf16),
            pltpu.VMEM((256, 256), bf16),
            pltpu.VMEM((8, top_rows, 256), f32),
            pltpu.VMEM((N_F, SUB, 128), f32),
            pltpu.VMEM((N_F, SUB, 128), f32),
            pltpu.VMEM((N_F, SUB, 128), f32),
            pltpu.VMEM((N_G, 16, SUB, 128), f32),
            pltpu.VMEM((FF // N_G, 128), f32),
            pltpu.VMEM((52, 8, 128), f32),
            pltpu.VMEM((52, 128), f32),
            pltpu.VMEM((FF // N_G, 128), bf16),
            dma((3,)),
            dma((count,)),
            dma((count,)),
            dma((count,)),
            dma((count,)),
            dma((4,)),
        ],
        compiler_params=pltpu.CompilerParams(
            collective_id=0, has_side_effects=True, vmem_limit_bytes=56 << 20
        ),
        name="rotate",
    )(weight, left, right)


def solution(mesh):
    in_specs = (P("fsdp", "grp"),)
    out_specs = (P("grp", "fsdp"), P("grp", "fsdp"))
    return jax.shard_map(body, mesh=mesh, in_specs=in_specs, out_specs=out_specs, check_vma=False)
```

```python
import functools
import math

import jax
import jax.numpy as jnp
import numpy as np
from jax import lax
from jax.experimental import pallas as pl
from jax.experimental.pallas import tpu as pltpu
from jax.sharding import PartitionSpec as P

MESH = pl.DeviceIdType.MESH
D = 8192
BLOCK = 128
FF = 26624
N_F = 64
N_G = 4
ROWS = FF // N_F
COLS = D // N_G
SUB = ROWS // 4
COEF = 1.0 / math.sqrt(FF * D)
SIZES = (8, 8, 16, 16, 16, 16, 8, 8, 8)
FINISH = 26


def paley_signs():
    squares_set = set()
    for coord_one in range(5):
        for coord_two in range(5):
            if coord_one or coord_two:
                squares_set.add(
                    (
                        (coord_one * coord_one + 2 * coord_two * coord_two) % 5,
                        2 * coord_one * coord_two % 5,
                    )
                )
    conference = np.zeros((26, 26), np.float32)
    conference[0, 1:] = 1.0
    conference[1:, 0] = 1.0
    for row_elem in range(25):
        for col_elem in range(25):
            diff_one = (row_elem % 5 - col_elem % 5) % 5
            diff_two = (row_elem // 5 - col_elem // 5) % 5
            if diff_one or diff_two:
                conference[1 + row_elem, 1 + col_elem] = (
                    1.0 if (diff_one, diff_two) in squares_set else -1.0
                )
    plus_block = np.array([[1.0, 1.0], [1.0, -1.0]], np.float32)
    minus_block = np.array([[1.0, -1.0], [-1.0, -1.0]], np.float32)
    return np.kron(conference, plus_block) + np.kron(np.eye(26), minus_block)


def sylvester(order):
    signs = np.ones((1, 1), np.float32)
    while signs.shape[0] < order:
        signs = np.kron(np.array([[1.0, 1.0], [1.0, -1.0]]), signs)
    return signs


def chunks():
    starts = np.cumsum((0,) + tuple(SIZES))
    return [(int(a), n) for a, n in zip(starts, SIZES)]


def butterflies(values):
    values = list(values)
    step = 1
    while step < len(values):
        for i in range(len(values)):
            if not i & step:
                a, b = values[i], values[i | step]
                values[i], values[i | step] = a + b, a - b
        step *= 2
    return values


def block_transpose(h, low_half, even_block):
    out = list(h)
    for a in (0, 1):
        t = pltpu.roll(jnp.where(low_half, h[a + 2], h[a]), 64, 1)
        out[a] = jnp.where(low_half, h[a], t)
        out[a + 2] = jnp.where(low_half, t, h[a + 2])
    h, out = out, list(out)
    for a in (0, 2):
        out[a] = jnp.where(even_block, h[a], pltpu.roll(h[a + 1], 32, 1))
        out[a + 1] = jnp.where(even_block, pltpu.roll(h[a], 96, 1), h[a + 1])
    return out


def kernel(
    w_hbm, l_hbm, s_hbm, o, m8,
    w, l, s256, x, s1, r1, z, g,
    load_sem, send1, recv1, send2, recv2,
):
    me_f, me_g = lax.axis_index("fsdp"), lax.axis_index("grp")
    all_chunks = chunks()
    loads = [
        pltpu.make_async_copy(src, dst, load_sem.at[i])
        for i, (src, dst) in enumerate(((w_hbm, w), (l_hbm, l), (s_hbm, s256)))
    ]
    for copy in loads:
        copy.start()

    me_x, me_z, me_y = me_f // 32, me_f // 4 % 8, me_f % 4
    z_at = [((me_z + dz) % 8) * 4 for dz in (0, 1, 7, 2, 6, 3, 5, 4)]

    def each_peer(dx, step):
        base = (me_x + dx) % 2 * 32

        def row(dy, low):
            p_y = base + (me_y + dy) % 4
            for at in z_at[low:]:
                step(p_y + at)

        if dx == 0:
            row(0, 1)

        @pl.loop(1 - dx, 4)
        def _(dy):
            row(dy, 0)

    def piece(r0, n, first, count=1):
        return pl.ds(pl.multiple_of(N_F * r0 + first * n, 8), count * n)

    barrier = pltpu.get_barrier_semaphore()

    def greet(p):
        pl.semaphore_signal(barrier, inc=1, device_id=(p, me_g), device_id_type=MESH)

    each_peer(1, greet)
    each_peer(0, greet)

    @pl.loop(1, N_G)
    def _(i):
        pl.semaphore_signal(barrier, inc=1, device_id=(me_f, (me_g + i) % N_G), device_id_type=MESH)

    lane = lax.broadcasted_iota(jnp.int32, (8, 128), 1)
    low_half = lane < 64
    even_block = (lane // 32) % 2 == 0
    m8[...] = jnp.zeros_like(m8)
    for copy in loads:
        copy.wait()

    def local_part(r0, n):
        lhs = l[4 * r0 : 4 * (r0 + n), :]
        for u in range(8):
            cols = slice(256 * u, 256 * (u + 1))
            part = jnp.dot(lhs, w[:, cols], preferred_element_type=jnp.float32)
            hi = part.astype(jnp.bfloat16)
            lo = (part - hi.astype(jnp.float32)).astype(jnp.bfloat16)
            x[u, : 4 * n, :] = jnp.dot(
                hi, s256[...], preferred_element_type=jnp.float32
            ) + jnp.dot(lo, s256[...], preferred_element_type=jnp.float32)

        @pl.loop(0, n // 8)
        def _(k):
            row = pl.multiple_of(k * 8, 8)
            for half in range(2):
                lanes = slice(128 * half, 128 * (half + 1))
                got = [
                    butterflies([x[u, pl.ds(row + a * n, 8), lanes] for u in range(8)])
                    for a in range(4)
                ]
                for u in range(8):
                    parts = block_transpose([got[a][u] for a in range(4)], low_half, even_block)
                    for b in range(4):
                        at = N_F * r0 + ((u * 2 + half) * 4 + b) * n + row
                        s1[pl.ds(pl.multiple_of(at, 8), 8), :] = parts[b]

    def send_fsdp(c, dx):
        r0, n = all_chunks[c]
        mine = piece(r0, n, me_f)
        if dx == 0:
            pltpu.make_async_copy(s1.at[mine], r1.at[mine], recv1.at[c]).start()

        def send(p):
            pltpu.make_async_remote_copy(
                src_ref=s1.at[piece(r0, n, p)],
                dst_ref=r1.at[mine],
                send_sem=send1.at[c],
                recv_sem=recv1.at[c],
                device_id=(p, me_g),
                device_id_type=MESH,
            ).start()

        each_peer(dx, send)

    def fsdp_part(c, r0, n):
        whole = r1.at[piece(r0, n, 0, N_F)]
        pltpu.make_async_copy(whole, whole, recv1.at[c]).wait()

        @pl.loop(0, n // 8)
        def _(k):
            def tile(i):
                return pl.ds(pl.multiple_of(N_F * r0 + i * n + k * 8, 8), 8)

            for a in range(8):
                got = butterflies([r1[tile(a * 8 + b), :] for b in range(8)])
                for b in range(8):
                    z[tile(a * 8 + b), :] = got[b]
            for b in range(8):
                got = butterflies([z[tile(a * 8 + b), :] for a in range(8)])
                for a in range(8):
                    z[tile(a * 8 + b), :] = got[a]

    def send_grp(c, r0, n):
        mine = piece(r0, n, me_g * 16, 16)
        pltpu.make_async_copy(z.at[mine], g.at[mine], recv2.at[c]).start()

        @pl.loop(1, N_G)
        def _(i):
            q = (me_g + i) % N_G
            pltpu.make_async_remote_copy(
                src_ref=z.at[piece(r0, n, q * 16, 16)],
                dst_ref=g.at[mine],
                send_sem=send2.at[c],
                recv_sem=recv2.at[c],
                device_id=(me_f, q),
                device_id_type=MESH,
            ).start()

    def grp_part(c, r0, n):
        whole = g.at[piece(r0, n, 0, N_F)]
        pltpu.make_async_copy(whole, whole, recv2.at[c]).wait()

        @pl.loop(0, 16)
        def _(m):
            for k in range(n // 8):
                tile = r0 // 8 + k
                got = butterflies(
                    [
                        g[pl.ds(pl.multiple_of(N_F * r0 + (a * 16 + m) * n + k * 8, 8), 8), :]
                        for a in range(4)
                    ]
                )
                parts = block_transpose(got, low_half, even_block)
                for b in range(4):
                    at = (m * 4 + b) * (SUB // 8) + tile
                    o[pl.ds(pl.multiple_of(at * 8, 8), 8), :] = parts[b]
                    m8[at // 16] = jnp.maximum(m8[at // 16], jnp.abs(parts[b]))

    last = len(all_chunks) - 1
    for c in range(last + 1):
        local_part(*all_chunks[c])
        if c == 0:
            pl.semaphore_wait(barrier, N_F + N_G - 2)
        send_fsdp(c, 1)
        send_fsdp(c, 0)
    for c in range(last + 1):
        fsdp_part(c, *all_chunks[c])
        send_grp(c, *all_chunks[c])
        if c:
            grp_part(c - 1, *all_chunks[c - 1])
    grp_part(last, *all_chunks[last])

    for c, (r0, n) in enumerate(all_chunks):
        sent = s1.at[piece(r0, n, 0, N_F - 1)]
        pltpu.make_async_copy(sent, sent, send1.at[c]).wait()
        sent = z.at[piece(r0, n, 0, 48)]
        pltpu.make_async_copy(sent, sent, send2.at[c]).wait()


def finish(o, m8, q_ref, scale_ref):
    first = pl.program_id(0) * FINISH
    lane = lax.broadcasted_iota(jnp.int32, scale_ref.shape, 1)
    tops = scale_ref[...]
    for i in range(FINISH):
        block = first + i
        top = jnp.max(jnp.max(m8[block], axis=0, keepdims=True), axis=1, keepdims=True) * COEF
        tops = jnp.where(lane == block, top, tops)
        rows = pl.ds(pl.multiple_of(block * BLOCK, BLOCK), BLOCK)
        q_ref[BLOCK * i : BLOCK * (i + 1), :] = (o[rows, :] * (COEF / (top + 1e-06))).astype(
            jnp.bfloat16
        )
    scale_ref[...] = tops


def body(weight):
    full = np.kron(sylvester(8), paley_signs())
    order = np.concatenate(
        [a * SUB + np.arange(r0, r0 + n) for r0, n in chunks() for a in range(4)]
    )
    left = jnp.asarray(full[order], jnp.bfloat16)
    right = jnp.asarray(sylvester(256), jnp.bfloat16)
    count = len(SIZES)
    f32, bf16 = jnp.float32, jnp.bfloat16
    rows_out = FF // N_G
    blocks = rows_out // BLOCK
    dma = pltpu.SemaphoreType.DMA
    mixed, tops = pl.pallas_call(
        kernel,
        out_shape=(pltpu.VMEM((rows_out, 128), f32), pltpu.VMEM((blocks, 8, 128), f32)),
        in_specs=[pl.BlockSpec(memory_space=pltpu.HBM)] * 3,
        out_specs=(pl.BlockSpec(memory_space=pltpu.VMEM),) * 2,
        scratch_shapes=[
            pltpu.VMEM((ROWS, COLS), bf16),
            pltpu.VMEM((ROWS, ROWS), bf16),
            pltpu.VMEM((256, 256), bf16),
            pltpu.VMEM((8, 4 * max(SIZES), 256), f32),
            *[pltpu.VMEM((N_F * SUB, 128), f32)] * 4,
            dma((3,)),
            *[dma((count,))] * 4,
        ],
        compiler_params=pltpu.CompilerParams(
            collective_id=0, has_side_effects=True, vmem_limit_bytes=60 << 20
        ),
        name="rotate",
    )(weight, left, right)
    quantized, scales = pl.pallas_call(
        finish,
        grid=(blocks // FINISH,),
        out_shape=(
            jax.ShapeDtypeStruct((rows_out, 128), bf16),
            jax.ShapeDtypeStruct((1, blocks), f32),
        ),
        in_specs=[pl.BlockSpec(memory_space=pltpu.VMEM)] * 2,
        out_specs=(
            pl.BlockSpec((FINISH * BLOCK, 128), lambda i: (i, 0)),
            pl.BlockSpec((1, blocks), lambda i: (0, 0)),
        ),
        compiler_params=pltpu.CompilerParams(vmem_limit_bytes=16 << 20),
        name="finish",
    )(mixed, tops)
    return quantized, scales.reshape(blocks, 1)


def solution(mesh):
    in_specs = (P("fsdp", "grp"),)
    out_specs = (P("grp", "fsdp"), P("grp", "fsdp"))
    return jax.shard_map(body, mesh=mesh, in_specs=in_specs, out_specs=out_specs, check_vma=False)
```

```python
import itertools
import math

import jax
import jax.numpy as jnp
import numpy as np
from jax import lax
from jax.experimental import pallas as pl
from jax.experimental.pallas import tpu as pltpu
from jax.sharding import PartitionSpec as P

MESH = pl.DeviceIdType.MESH
D = 8192
BLOCK = 128
FF = 26624
N_F = 64
N_G = 4
ROWS = FF // N_F
COLS = D // N_G
SUB = ROWS // 4
COEF = 1.0 / math.sqrt(FF * D)
SIZES = (8, 8, 16, 16, 16, 16, 8, 8, 8)
FINISH = 26
Z_ORDER = (1, 7, 2, 6, 3, 5, 4, 0)
LEAD = 4
LAG = 1
GROUP = 4


def paley_signs():
    squares_set = set()
    for coord_one in range(5):
        for coord_two in range(5):
            if coord_one or coord_two:
                squares_set.add(
                    (
                        (coord_one * coord_one + 2 * coord_two * coord_two) % 5,
                        2 * coord_one * coord_two % 5,
                    )
                )
    conference = np.zeros((26, 26), np.float32)
    conference[0, 1:] = 1.0
    conference[1:, 0] = 1.0
    for row_elem in range(25):
        for col_elem in range(25):
            diff_one = (row_elem % 5 - col_elem % 5) % 5
            diff_two = (row_elem // 5 - col_elem // 5) % 5
            if diff_one or diff_two:
                conference[1 + row_elem, 1 + col_elem] = (
                    1.0 if (diff_one, diff_two) in squares_set else -1.0
                )
    plus_block = np.array([[1.0, 1.0], [1.0, -1.0]], np.float32)
    minus_block = np.array([[1.0, -1.0], [-1.0, -1.0]], np.float32)
    return np.kron(conference, plus_block) + np.kron(np.eye(26), minus_block)


def sylvester(order):
    signs = np.ones((1, 1), np.float32)
    while signs.shape[0] < order:
        signs = np.kron(np.array([[1.0, 1.0], [1.0, -1.0]]), signs)
    return signs


def chunks():
    starts = np.cumsum((0,) + tuple(SIZES))
    return [(int(a), n) for a, n in zip(starts, SIZES)]


def butterflies(values):
    values = list(values)
    step = 1
    while step < len(values):
        for i in range(len(values)):
            if not i & step:
                a, b = values[i], values[i | step]
                values[i], values[i | step] = a + b, a - b
        step *= 2
    return values


def block_transpose(h, low_half, even_block):
    out = list(h)
    for a in (0, 1):
        t = pltpu.roll(jnp.where(low_half, h[a + 2], h[a]), 64, 1)
        out[a] = jnp.where(low_half, h[a], t)
        out[a + 2] = jnp.where(low_half, t, h[a + 2])
    h, out = out, list(out)
    for a in (0, 2):
        out[a] = jnp.where(even_block, h[a], pltpu.roll(h[a + 1], 32, 1))
        out[a + 1] = jnp.where(even_block, pltpu.roll(h[a], 96, 1), h[a + 1])
    return out


def kernel(
    w_hbm, l_hbm, s_hbm, o,
    w, l, s256, x, s1, r1, z, g,
    load_sem, send1, recv1, send2, recv2,
):
    me_f, me_g = lax.axis_index("fsdp"), lax.axis_index("grp")
    all_chunks = chunks()
    loads = [
        pltpu.make_async_copy(src, dst, load_sem.at[i])
        for i, (src, dst) in enumerate(((w_hbm, w), (l_hbm, l), (s_hbm, s256)))
    ]
    for copy in loads:
        copy.start()

    me_x, me_z, me_y = me_f // 32, me_f // 4 % 8, me_f % 4
    z_at = [((me_z + dz) % 8) * 4 for dz in Z_ORDER]

    def each_peer(dx, step):
        base = (me_x + dx) % 2 * 32

        def row(dy, ats):
            p_y = base + (me_y + dy) % 4
            for at in ats:
                step(p_y + at)

        @pl.loop(0, 3)
        def _(i):
            row(2 + i + i // 2, z_at)

        row(0, z_at if dx else z_at[:-1])

    def piece(r0, n, first, count=1):
        return pl.ds(pl.multiple_of(N_F * r0 + first * n, 8), count * n)

    barrier = pltpu.get_barrier_semaphore()

    def greet(p):
        pl.semaphore_signal(barrier, inc=1, device_id=(p, me_g), device_id_type=MESH)

    each_peer(1, greet)
    each_peer(0, greet)

    @pl.loop(1, N_G)
    def _(i):
        pl.semaphore_signal(barrier, inc=1, device_id=(me_f, (me_g + i) % N_G), device_id_type=MESH)

    lane = lax.broadcasted_iota(jnp.int32, (8, 128), 1)
    low_half = lane < 64
    even_block = (lane // 32) % 2 == 0
    for copy in loads:
        copy.wait()

    def local_part(r0, n):
        lhs = l[4 * r0 : 4 * (r0 + n), :]
        for u in range(8):
            cols = slice(256 * u, 256 * (u + 1))
            part = jnp.dot(lhs, w[:, cols], preferred_element_type=jnp.float32)
            hi = part.astype(jnp.bfloat16)
            lo = (part - hi.astype(jnp.float32)).astype(jnp.bfloat16)
            x[u, : 4 * n, :] = jnp.dot(
                hi, s256[...], preferred_element_type=jnp.float32
            ) + jnp.dot(lo, s256[...], preferred_element_type=jnp.float32)

        @pl.loop(0, n // 8)
        def _(k):
            row = pl.multiple_of(k * 8, 8)
            for half in range(2):
                lanes = slice(128 * half, 128 * (half + 1))
                got = [
                    butterflies([x[u, pl.ds(row + a * n, 8), lanes] for u in range(8)])
                    for a in range(4)
                ]
                for u in range(8):
                    parts = block_transpose([got[a][u] for a in range(4)], low_half, even_block)
                    for b in range(4):
                        at = N_F * r0 + ((u * 2 + half) * 4 + b) * n + row
                        s1[pl.ds(pl.multiple_of(at, 8), 8), :] = parts[b]

    def send_fsdp(c, dx):
        r0, n = all_chunks[c]
        mine = piece(r0, n, me_f)
        if dx == 0:
            pltpu.make_async_copy(s1.at[mine], r1.at[mine], recv1.at[c]).start()

        def send(p):
            pltpu.make_async_remote_copy(
                src_ref=s1.at[piece(r0, n, p)],
                dst_ref=r1.at[mine],
                send_sem=send1.at[c],
                recv_sem=recv1.at[c],
                device_id=(p, me_g),
                device_id_type=MESH,
            ).start()

        each_peer(dx, send)

    def fsdp_part(c, r0, n):
        whole = r1.at[piece(r0, n, 0, N_F)]
        pltpu.make_async_copy(whole, whole, recv1.at[c]).wait()

        @pl.loop(0, n // 8)
        def _(k):
            def tile(i):
                return pl.ds(pl.multiple_of(N_F * r0 + i * n + k * 8, 8), 8)

            for a in range(8):
                got = butterflies([r1[tile(a * 8 + b), :] for b in range(8)])
                for b in range(8):
                    z[tile(a * 8 + b), :] = got[b]
            for b in range(8):
                got = butterflies([z[tile(a * 8 + b), :] for a in range(8)])
                for a in range(8):
                    z[tile(a * 8 + b), :] = got[a]

    def send_grp(c, r0, n):
        mine = piece(r0, n, me_g * 16, 16)
        pltpu.make_async_copy(z.at[mine], g.at[mine], recv2.at[c]).start()

        def send(q):
            pltpu.make_async_remote_copy(
                src_ref=z.at[piece(r0, n, q * 16, 16)],
                dst_ref=g.at[mine],
                send_sem=send2.at[c],
                recv_sem=recv2.at[c],
                device_id=(me_f, q),
                device_id_type=MESH,
            ).start()

        core, chip = me_g % 2, me_g // 2
        send((1 - chip) * 2 + core)
        send((1 - chip) * 2 + 1 - core)
        send(chip * 2 + 1 - core)

    def grp_part(c, r0, n):
        whole = g.at[piece(r0, n, 0, N_F)]
        pltpu.make_async_copy(whole, whole, recv2.at[c]).wait()

        @pl.loop(0, 16 // GROUP)
        def _(step):
            done = []
            for m, k in itertools.product(range(GROUP), range(n // 8)):
                m = step * GROUP + m
                got = butterflies(
                    [
                        g[pl.ds(pl.multiple_of(N_F * r0 + (a * 16 + m) * n + k * 8, 8), 8), :]
                        for a in range(4)
                    ]
                )
                at = m * 4 * SUB + r0 + k * 8
                done.append((at, block_transpose(got, low_half, even_block)))
            for at, parts in done:
                for b in range(4):
                    o[pl.ds(pl.multiple_of(at + b * SUB, 8), 8), :] = parts[b]

    count = len(all_chunks)
    for step in range(-LEAD, count + LAG):
        if 0 <= step < count:
            fsdp_part(step, *all_chunks[step])
            send_grp(step, *all_chunks[step])
        if step + LEAD < count:
            local_part(*all_chunks[step + LEAD])
            if step == -LEAD:
                pl.semaphore_wait(barrier, N_F + N_G - 2)
            send_fsdp(step + LEAD, 1)
            send_fsdp(step + LEAD, 0)
        if step >= LAG:
            grp_part(step - LAG, *all_chunks[step - LAG])
    for c, (r0, n) in enumerate(all_chunks):
        sent = s1.at[piece(r0, n, 0, N_F - 1)]
        pltpu.make_async_copy(sent, sent, send1.at[c]).wait()
        sent = z.at[piece(r0, n, 0, 48)]
        pltpu.make_async_copy(sent, sent, send2.at[c]).wait()


def finish(o, q_ref, scale_ref):
    first = pl.program_id(0) * FINISH
    lane = lax.broadcasted_iota(jnp.int32, scale_ref.shape, 1)
    tops = scale_ref[...]
    for i in range(FINISH):
        block = first + i
        values = o[pl.ds(pl.multiple_of(block * BLOCK, BLOCK), BLOCK), :]
        top = jnp.max(jnp.max(jnp.abs(values), axis=0, keepdims=True), axis=1, keepdims=True)
        top = top * COEF
        tops = jnp.where(lane == block, top, tops)
        q_ref[BLOCK * i : BLOCK * (i + 1), :] = (values * (COEF / (top + 1e-06))).astype(
            jnp.bfloat16
        )
    scale_ref[...] = tops


def body(weight):
    full = np.kron(sylvester(8), paley_signs())
    order = np.concatenate(
        [a * SUB + np.arange(r0, r0 + n) for r0, n in chunks() for a in range(4)]
    )
    left = jnp.asarray(full[order], jnp.bfloat16)
    right = jnp.asarray(sylvester(256), jnp.bfloat16)
    count = len(SIZES)
    f32, bf16 = jnp.float32, jnp.bfloat16
    rows_out = FF // N_G
    blocks = rows_out // BLOCK
    dma = pltpu.SemaphoreType.DMA
    mixed = pl.pallas_call(
        kernel,
        out_shape=pltpu.VMEM((rows_out, 128), f32),
        in_specs=[pl.BlockSpec(memory_space=pltpu.HBM)] * 3,
        out_specs=pl.BlockSpec(memory_space=pltpu.VMEM),
        scratch_shapes=[
            pltpu.VMEM((ROWS, COLS), bf16),
            pltpu.VMEM((ROWS, ROWS), bf16),
            pltpu.VMEM((256, 256), bf16),
            pltpu.VMEM((8, 4 * max(SIZES), 256), f32),
            *[pltpu.VMEM((N_F * SUB, 128), f32)] * 4,
            dma((3,)),
            *[dma((count,))] * 4,
        ],
        compiler_params=pltpu.CompilerParams(
            collective_id=0, has_side_effects=True, vmem_limit_bytes=60 << 20
        ),
        name="rotate",
    )(weight, left, right)
    quantized, scales = pl.pallas_call(
        finish,
        grid=(blocks // FINISH,),
        out_shape=(
            jax.ShapeDtypeStruct((rows_out, 128), bf16),
            jax.ShapeDtypeStruct((1, blocks), f32),
        ),
        in_specs=[pl.BlockSpec(memory_space=pltpu.VMEM)],
        out_specs=(
            pl.BlockSpec((FINISH * BLOCK, 128), lambda i: (i, 0)),
            pl.BlockSpec((1, blocks), lambda i: (0, 0)),
        ),
        compiler_params=pltpu.CompilerParams(vmem_limit_bytes=16 << 20),
        name="finish",
    )(mixed)
    return quantized, scales.reshape(blocks, 1)


def solution(mesh):
    in_specs = (P("fsdp", "grp"),)
    out_specs = (P("grp", "fsdp"), P("grp", "fsdp"))
    return jax.shard_map(body, mesh=mesh, in_specs=in_specs, out_specs=out_specs, check_vma=False)
```

```python
import itertools
import math

import jax
import jax.numpy as jnp
import numpy as np
from jax import lax
from jax.experimental import pallas as pl
from jax.experimental.pallas import tpu as pltpu
from jax.sharding import PartitionSpec as P

MESH = pl.DeviceIdType.MESH
D = 8192
BLOCK = 128
FF = 26624
N_F = 64
N_G = 4
ROWS = FF // N_F
COLS = D // N_G
SUB = ROWS // 4
COEF = 1.0 / math.sqrt(FF * D)
SIZES = (8, 8, 16, 16, 16, 16, 8, 8, 8)
FINISH = 26
Z_ORDER = (1, 7, 2, 6, 3, 5, 4, 0)
LEAD = 4
LAG = 1
GROUP = 4


def paley_signs():
    squares_set = set()
    for coord_one in range(5):
        for coord_two in range(5):
            if coord_one or coord_two:
                squares_set.add(
                    (
                        (coord_one * coord_one + 2 * coord_two * coord_two) % 5,
                        2 * coord_one * coord_two % 5,
                    )
                )
    conference = np.zeros((26, 26), np.float32)
    conference[0, 1:] = 1.0
    conference[1:, 0] = 1.0
    for row_elem in range(25):
        for col_elem in range(25):
            diff_one = (row_elem % 5 - col_elem % 5) % 5
            diff_two = (row_elem // 5 - col_elem // 5) % 5
            if diff_one or diff_two:
                conference[1 + row_elem, 1 + col_elem] = (
                    1.0 if (diff_one, diff_two) in squares_set else -1.0
                )
    plus_block = np.array([[1.0, 1.0], [1.0, -1.0]], np.float32)
    minus_block = np.array([[1.0, -1.0], [-1.0, -1.0]], np.float32)
    return np.kron(conference, plus_block) + np.kron(np.eye(26), minus_block)


def sylvester(order):
    signs = np.ones((1, 1), np.float32)
    while signs.shape[0] < order:
        signs = np.kron(np.array([[1.0, 1.0], [1.0, -1.0]]), signs)
    return signs


def chunks():
    starts = np.cumsum((0,) + tuple(SIZES))
    return [(int(a), n) for a, n in zip(starts, SIZES)]


def butterflies(values):
    values = list(values)
    step = 1
    while step < len(values):
        for i in range(len(values)):
            if not i & step:
                a, b = values[i], values[i | step]
                values[i], values[i | step] = a + b, a - b
        step *= 2
    return values


def block_transpose(h, low_half, even_block):
    out = list(h)
    for a in (0, 1):
        t = pltpu.roll(jnp.where(low_half, h[a + 2], h[a]), 64, 1)
        out[a] = jnp.where(low_half, h[a], t)
        out[a + 2] = jnp.where(low_half, t, h[a + 2])
    h, out = out, list(out)
    for a in (0, 2):
        out[a] = jnp.where(even_block, h[a], pltpu.roll(h[a + 1], 32, 1))
        out[a + 1] = jnp.where(even_block, pltpu.roll(h[a], 96, 1), h[a + 1])
    return out


def kernel(
    w_hbm, l_hbm, s_hbm, o,
    w, l, s256, x, s1, r1, z, g,
    load_sem, send1, recv1, send2, recv2,
):
    me_f, me_g = lax.axis_index("fsdp"), lax.axis_index("grp")
    all_chunks = chunks()
    loads = [
        pltpu.make_async_copy(src, dst, load_sem.at[i])
        for i, (src, dst) in enumerate(((w_hbm, w), (l_hbm, l), (s_hbm, s256)))
    ]
    for copy in loads:
        copy.start()

    me_x, me_z, me_y = me_f // 32, me_f // 4 % 8, me_f % 4
    z_at = [((me_z + dz) % 8) * 4 for dz in Z_ORDER]

    def each_peer(dx, step, ats):
        base = (me_x + dx) % 2 * 32

        def row(dy, ats):
            p_y = base + (me_y + dy) % 4
            for at in ats:
                step(p_y + at)

        @pl.loop(0, 3)
        def _(i):
            row(2 + i + i // 2, [*ats, z_at[-1]])

        row(0, [*ats, z_at[-1]] if dx else ats)

    def piece(r0, n, first, count=1):
        return pl.ds(pl.multiple_of(N_F * r0 + first * n, 8), count * n)

    barrier = pltpu.get_barrier_semaphore()

    def greet(p):
        pl.semaphore_signal(barrier, inc=1, device_id=(p, me_g), device_id_type=MESH)

    each_peer(1, greet, z_at[-2::-1])
    each_peer(0, greet, z_at[-2::-1])

    @pl.loop(1, N_G)
    def _(i):
        pl.semaphore_signal(barrier, inc=1, device_id=(me_f, (me_g + i) % N_G), device_id_type=MESH)

    lane = lax.broadcasted_iota(jnp.int32, (8, 128), 1)
    low_half = lane < 64
    even_block = (lane // 32) % 2 == 0
    for copy in loads:
        copy.wait()

    def local_part(r0, n):
        lhs = l[4 * r0 : 4 * (r0 + n), :]
        for u in range(8):
            cols = slice(256 * u, 256 * (u + 1))
            part = jnp.dot(lhs, w[:, cols], preferred_element_type=jnp.float32)
            hi = part.astype(jnp.bfloat16)
            lo = (part - hi.astype(jnp.float32)).astype(jnp.bfloat16)
            x[u, : 4 * n, :] = jnp.dot(
                hi, s256[...], preferred_element_type=jnp.float32
            ) + jnp.dot(lo, s256[...], preferred_element_type=jnp.float32)

        @pl.loop(0, n // 8)
        def _(k):
            row = pl.multiple_of(k * 8, 8)
            for half in range(2):
                lanes = slice(128 * half, 128 * (half + 1))
                got = [
                    butterflies([x[u, pl.ds(row + a * n, 8), lanes] for u in range(8)])
                    for a in range(4)
                ]
                for u in range(8):
                    parts = block_transpose([got[a][u] for a in range(4)], low_half, even_block)
                    for b in range(4):
                        at = N_F * r0 + ((u * 2 + half) * 4 + b) * n + row
                        s1[pl.ds(pl.multiple_of(at, 8), 8), :] = parts[b]

    def send_fsdp(c, dx):
        r0, n = all_chunks[c]
        mine = piece(r0, n, me_f)
        if dx == 0:
            pltpu.make_async_copy(s1.at[mine], r1.at[mine], recv1.at[c]).start()

        def send(p):
            pltpu.make_async_remote_copy(
                src_ref=s1.at[piece(r0, n, p)],
                dst_ref=r1.at[mine],
                send_sem=send1.at[c],
                recv_sem=recv1.at[c],
                device_id=(p, me_g),
                device_id_type=MESH,
            ).start()

        each_peer(dx, send, z_at[:-1])

    def fsdp_part(c, r0, n):
        whole = r1.at[piece(r0, n, 0, N_F)]
        pltpu.make_async_copy(whole, whole, recv1.at[c]).wait()

        def tile(i, k):
            return pl.ds(pl.multiple_of(N_F * r0 + i * n + k * 8, 8), 8)

        @pl.loop(0, n // 8)
        def _(k):
            for b in range(8):
                got = butterflies([r1[tile(a * 8 + b, k), :] for a in range(8)])
                for a in range(8):
                    z[tile(a * 8 + b, k), :] = got[a]

        mine = piece(r0, n, me_g * 16, 16)

        def block(q):
            for k in range(n // 8):
                for a in range(2):
                    at = [tile(q * 16 + a * 8 + b, k) for b in range(8)]
                    got = butterflies([z[i, :] for i in at])
                    for i, value in zip(at, got):
                        z[i, :] = value

        def send(q):
            block(q)
            pltpu.make_async_remote_copy(
                src_ref=z.at[piece(r0, n, q * 16, 16)],
                dst_ref=g.at[mine],
                send_sem=send2.at[c],
                recv_sem=recv2.at[c],
                device_id=(me_f, q),
                device_id_type=MESH,
            ).start()

        core, chip = me_g % 2, me_g // 2
        send((1 - chip) * 2 + core)
        send((1 - chip) * 2 + 1 - core)
        send(chip * 2 + 1 - core)
        block(me_g)
        pltpu.make_async_copy(z.at[mine], g.at[mine], recv2.at[c]).start()

    def grp_part(c, r0, n):
        whole = g.at[piece(r0, n, 0, N_F)]
        pltpu.make_async_copy(whole, whole, recv2.at[c]).wait()

        @pl.loop(0, 16 // GROUP)
        def _(step):
            done = []
            for m, k in itertools.product(range(GROUP), range(n // 8)):
                m = step * GROUP + m
                got = butterflies(
                    [
                        g[pl.ds(pl.multiple_of(N_F * r0 + (a * 16 + m) * n + k * 8, 8), 8), :]
                        for a in range(4)
                    ]
                )
                at = m * 4 * SUB + r0 + k * 8
                done.append((at, block_transpose(got, low_half, even_block)))
            for at, parts in done:
                for b in range(4):
                    o[pl.ds(pl.multiple_of(at + b * SUB, 8), 8), :] = parts[b]

    count = len(all_chunks)
    for step in range(-LEAD, count + LAG):
        if 0 <= step < count:
            fsdp_part(step, *all_chunks[step])
        if step + LEAD < count:
            local_part(*all_chunks[step + LEAD])
            if step == -LEAD:
                pl.semaphore_wait(barrier, N_F + N_G - 2)
            send_fsdp(step + LEAD, 1)
            send_fsdp(step + LEAD, 0)
        if step >= LAG:
            grp_part(step - LAG, *all_chunks[step - LAG])
    for c, (r0, n) in enumerate(all_chunks):
        sent = s1.at[piece(r0, n, 0, N_F - 1)]
        pltpu.make_async_copy(sent, sent, send1.at[c]).wait()
        sent = z.at[piece(r0, n, 0, 48)]
        pltpu.make_async_copy(sent, sent, send2.at[c]).wait()


def finish(o, q_ref, scale_ref):
    first = pl.program_id(0) * FINISH
    lane = lax.broadcasted_iota(jnp.int32, scale_ref.shape, 1)
    tops = scale_ref[...]
    for i in range(FINISH):
        block = first + i
        values = o[pl.ds(pl.multiple_of(block * BLOCK, BLOCK), BLOCK), :]
        top = jnp.max(jnp.max(jnp.abs(values), axis=0, keepdims=True), axis=1, keepdims=True)
        top = top * COEF
        tops = jnp.where(lane == block, top, tops)
        q_ref[BLOCK * i : BLOCK * (i + 1), :] = (values * (COEF / (top + 1e-06))).astype(
            jnp.bfloat16
        )
    scale_ref[...] = tops


def body(weight):
    full = np.kron(sylvester(8), paley_signs())
    order = np.concatenate(
        [a * SUB + np.arange(r0, r0 + n) for r0, n in chunks() for a in range(4)]
    )
    left = jnp.asarray(full[order], jnp.bfloat16)
    right = jnp.asarray(sylvester(256), jnp.bfloat16)
    count = len(SIZES)
    f32, bf16 = jnp.float32, jnp.bfloat16
    rows_out = FF // N_G
    blocks = rows_out // BLOCK
    dma = pltpu.SemaphoreType.DMA
    mixed = pl.pallas_call(
        kernel,
        out_shape=pltpu.VMEM((rows_out, 128), f32),
        in_specs=[pl.BlockSpec(memory_space=pltpu.HBM)] * 3,
        out_specs=pl.BlockSpec(memory_space=pltpu.VMEM),
        scratch_shapes=[
            pltpu.VMEM((ROWS, COLS), bf16),
            pltpu.VMEM((ROWS, ROWS), bf16),
            pltpu.VMEM((256, 256), bf16),
            pltpu.VMEM((8, 4 * max(SIZES), 256), f32),
            *[pltpu.VMEM((N_F * SUB, 128), f32)] * 4,
            dma((3,)),
            *[dma((count,))] * 4,
        ],
        compiler_params=pltpu.CompilerParams(
            collective_id=0, has_side_effects=True, vmem_limit_bytes=60 << 20
        ),
        name="rotate",
    )(weight, left, right)
    quantized, scales = pl.pallas_call(
        finish,
        grid=(blocks // FINISH,),
        out_shape=(
            jax.ShapeDtypeStruct((rows_out, 128), bf16),
            jax.ShapeDtypeStruct((1, blocks), f32),
        ),
        in_specs=[pl.BlockSpec(memory_space=pltpu.VMEM)],
        out_specs=(
            pl.BlockSpec((FINISH * BLOCK, 128), lambda i: (i, 0)),
            pl.BlockSpec((1, blocks), lambda i: (0, 0)),
        ),
        compiler_params=pltpu.CompilerParams(vmem_limit_bytes=16 << 20),
        name="finish",
    )(mixed)
    return quantized, scales.reshape(blocks, 1)


def solution(mesh):
    in_specs = (P("fsdp", "grp"),)
    out_specs = (P("grp", "fsdp"), P("grp", "fsdp"))
    return jax.shard_map(body, mesh=mesh, in_specs=in_specs, out_specs=out_specs, check_vma=False)
```

```python
import itertools
import math

import jax
import jax.numpy as jnp
import numpy as np
from jax import lax
from jax.experimental import pallas as pl
from jax.experimental.pallas import tpu as pltpu
from jax.sharding import PartitionSpec as P

MESH = pl.DeviceIdType.MESH
D = 8192
BLOCK = 128
FF = 26624
N_F = 64
N_G = 4
ROWS = FF // N_F
COLS = D // N_G
SUB = ROWS // 4
COEF = 1.0 / math.sqrt(FF * D)
SIZES = (8, 8, 16, 16, 16, 16, 8, 8, 8)
FINISH = 13
Z_ORDER = (1, 7, 2, 6, 3, 5, 4, 0)
LEAD = 4
LAG = 1
GROUP = 4


def paley_signs():
    squares_set = set()
    for coord_one in range(5):
        for coord_two in range(5):
            if coord_one or coord_two:
                squares_set.add(
                    (
                        (coord_one * coord_one + 2 * coord_two * coord_two) % 5,
                        2 * coord_one * coord_two % 5,
                    )
                )
    conference = np.zeros((26, 26), np.float32)
    conference[0, 1:] = 1.0
    conference[1:, 0] = 1.0
    for row_elem in range(25):
        for col_elem in range(25):
            diff_one = (row_elem % 5 - col_elem % 5) % 5
            diff_two = (row_elem // 5 - col_elem // 5) % 5
            if diff_one or diff_two:
                conference[1 + row_elem, 1 + col_elem] = (
                    1.0 if (diff_one, diff_two) in squares_set else -1.0
                )
    plus_block = np.array([[1.0, 1.0], [1.0, -1.0]], np.float32)
    minus_block = np.array([[1.0, -1.0], [-1.0, -1.0]], np.float32)
    return np.kron(conference, plus_block) + np.kron(np.eye(26), minus_block)


def sylvester(order):
    signs = np.ones((1, 1), np.float32)
    while signs.shape[0] < order:
        signs = np.kron(np.array([[1.0, 1.0], [1.0, -1.0]]), signs)
    return signs


def chunks():
    starts = np.cumsum((0,) + tuple(SIZES))
    return [(int(a), n) for a, n in zip(starts, SIZES)]


def butterflies(values):
    values = list(values)
    step = 1
    while step < len(values):
        for i in range(len(values)):
            if not i & step:
                a, b = values[i], values[i | step]
                values[i], values[i | step] = a + b, a - b
        step *= 2
    return values


def block_transpose(h, low_half, even_block):
    out = list(h)
    for a in (0, 1):
        t = pltpu.roll(jnp.where(low_half, h[a + 2], h[a]), 64, 1)
        out[a] = jnp.where(low_half, h[a], t)
        out[a + 2] = jnp.where(low_half, t, h[a + 2])
    h, out = out, list(out)
    for a in (0, 2):
        out[a] = jnp.where(even_block, h[a], pltpu.roll(h[a + 1], 32, 1))
        out[a + 1] = jnp.where(even_block, pltpu.roll(h[a], 96, 1), h[a + 1])
    return out


def kernel(
    w_hbm, l_hbm, s_hbm, o,
    w, l, s256, x, s1, r1, z, g,
    load_sem, send1, recv1, send2, recv2,
):
    me_f, me_g = lax.axis_index("fsdp"), lax.axis_index("grp")
    all_chunks = chunks()
    loads = [
        pltpu.make_async_copy(src, dst, load_sem.at[i])
        for i, (src, dst) in enumerate(((w_hbm, w), (l_hbm, l), (s_hbm, s256)))
    ]
    for copy in loads:
        copy.start()

    me_x, me_z, me_y = me_f // 32, me_f // 4 % 8, me_f % 4
    z_at = [((me_z + dz) % 8) * 4 for dz in Z_ORDER]

    def each_peer(dx, step):
        base = (me_x + dx) % 2 * 32

        def row(dy, ats):
            p_y = base + (me_y + dy) % 4
            for at in ats:
                step(p_y + at)

        @pl.loop(0, 3)
        def _(i):
            row(2 + i + i // 2, z_at)

        row(0, z_at if dx else z_at[:-1])

    def piece(r0, n, first, count=1):
        return pl.ds(pl.multiple_of(N_F * r0 + first * n, 8), count * n)

    barrier = pltpu.get_barrier_semaphore()

    def greet(p):
        pl.semaphore_signal(barrier, inc=1, device_id=(p, me_g), device_id_type=MESH)

    each_peer(1, greet)
    each_peer(0, greet)

    @pl.loop(1, N_G)
    def _(i):
        pl.semaphore_signal(barrier, inc=1, device_id=(me_f, (me_g + i) % N_G), device_id_type=MESH)

    lane = lax.broadcasted_iota(jnp.int32, (8, 128), 1)
    low_half = lane < 64
    even_block = (lane // 32) % 2 == 0
    for copy in loads:
        copy.wait()

    def local_part(r0, n):
        lhs = l[4 * r0 : 4 * (r0 + n), :]
        for u in range(8):
            cols = slice(256 * u, 256 * (u + 1))
            part = jnp.dot(lhs, w[:, cols], preferred_element_type=jnp.float32)
            hi = part.astype(jnp.bfloat16)
            lo = (part - hi.astype(jnp.float32)).astype(jnp.bfloat16)
            x[u, : 4 * n, :] = jnp.dot(
                hi, s256[...], preferred_element_type=jnp.float32
            ) + jnp.dot(lo, s256[...], preferred_element_type=jnp.float32)

        @pl.loop(0, n // 8)
        def _(k):
            row = pl.multiple_of(k * 8, 8)
            for half in range(2):
                lanes = slice(128 * half, 128 * (half + 1))
                got = [
                    butterflies([x[u, pl.ds(row + a * n, 8), lanes] for u in range(8)])
                    for a in range(4)
                ]
                for u in range(8):
                    parts = block_transpose([got[a][u] for a in range(4)], low_half, even_block)
                    for b in range(4):
                        at = N_F * r0 + ((u * 2 + half) * 4 + b) * n + row
                        s1[pl.ds(pl.multiple_of(at, 8), 8), :] = parts[b]

    def send_fsdp(c, dx):
        r0, n = all_chunks[c]
        mine = piece(r0, n, me_f)
        if dx == 0:
            pltpu.make_async_copy(s1.at[mine], r1.at[mine], recv1.at[c]).start()

        def send(p):
            pltpu.make_async_remote_copy(
                src_ref=s1.at[piece(r0, n, p)],
                dst_ref=r1.at[mine],
                send_sem=send1.at[c],
                recv_sem=recv1.at[c],
                device_id=(p, me_g),
                device_id_type=MESH,
            ).start()

        each_peer(dx, send)

    def fsdp_part(c, r0, n):
        whole = r1.at[piece(r0, n, 0, N_F)]
        pltpu.make_async_copy(whole, whole, recv1.at[c]).wait()

        @pl.loop(0, n // 8)
        def _(k):
            def tile(i):
                return pl.ds(pl.multiple_of(N_F * r0 + i * n + k * 8, 8), 8)

            for a in range(8):
                got = butterflies([r1[tile(a * 8 + b), :] for b in range(8)])
                for b in range(8):
                    z[tile(a * 8 + b), :] = got[b]
            for b in range(8):
                got = butterflies([z[tile(a * 8 + b), :] for a in range(8)])
                for a in range(8):
                    z[tile(a * 8 + b), :] = got[a]

    def send_grp(c, r0, n):
        mine = piece(r0, n, me_g * 16, 16)
        pltpu.make_async_copy(z.at[mine], g.at[mine], recv2.at[c]).start()

        def send(q):
            pltpu.make_async_remote_copy(
                src_ref=z.at[piece(r0, n, q * 16, 16)],
                dst_ref=g.at[mine],
                send_sem=send2.at[c],
                recv_sem=recv2.at[c],
                device_id=(me_f, q),
                device_id_type=MESH,
            ).start()

        core, chip = me_g % 2, me_g // 2
        send((1 - chip) * 2 + core)
        send((1 - chip) * 2 + 1 - core)
        send(chip * 2 + 1 - core)

    def grp_part(c, r0, n):
        whole = g.at[piece(r0, n, 0, N_F)]
        pltpu.make_async_copy(whole, whole, recv2.at[c]).wait()

        @pl.loop(0, 16 // GROUP)
        def _(step):
            done = []
            for m, k in itertools.product(range(GROUP), range(n // 8)):
                m = step * GROUP + m
                got = butterflies(
                    [
                        g[pl.ds(pl.multiple_of(N_F * r0 + (a * 16 + m) * n + k * 8, 8), 8), :]
                        for a in range(4)
                    ]
                )
                at = m * 4 * SUB + r0 + k * 8
                done.append((at, block_transpose(got, low_half, even_block)))
            for at, parts in done:
                for b in range(4):
                    o[pl.ds(pl.multiple_of(at + b * SUB, 8), 8), :] = parts[b]

    count = len(all_chunks)
    for step in range(-LEAD, count + LAG):
        if 0 <= step < count:
            fsdp_part(step, *all_chunks[step])
            send_grp(step, *all_chunks[step])
        if step + LEAD < count:
            local_part(*all_chunks[step + LEAD])
            if step == -LEAD:
                pl.semaphore_wait(barrier, N_F + N_G - 2)
            send_fsdp(step + LEAD, 1)
            send_fsdp(step + LEAD, 0)
        if step >= LAG:
            grp_part(step - LAG, *all_chunks[step - LAG])
    for c, (r0, n) in enumerate(all_chunks):
        sent = s1.at[piece(r0, n, 0, N_F - 1)]
        pltpu.make_async_copy(sent, sent, send1.at[c]).wait()
        sent = z.at[piece(r0, n, 0, 48)]
        pltpu.make_async_copy(sent, sent, send2.at[c]).wait()


def finish(o, q_hbm, scale_ref, qv, sems):
    lane = lax.broadcasted_iota(jnp.int32, scale_ref.shape, 1)
    tops = jnp.zeros(scale_ref.shape, jnp.float32)
    copies = []
    for block in range(scale_ref.shape[1]):
        rows = slice(BLOCK * block, BLOCK * (block + 1))
        values = o[rows, :]
        top = jnp.max(jnp.max(jnp.abs(values), axis=0, keepdims=True), axis=1, keepdims=True)
        top = top * COEF
        tops = jnp.where(lane == block, top, tops)
        qv[rows, :] = (values * (COEF / (top + 1e-06))).astype(jnp.bfloat16)
        if (block + 1) % FINISH == 0:
            part = block // FINISH
            done = pl.ds(part * FINISH * BLOCK, FINISH * BLOCK)
            copies.append(pltpu.make_async_copy(qv.at[done], q_hbm.at[done], sems.at[part]))
            copies[-1].start()
    scale_ref[...] = tops
    for copy in copies:
        copy.wait()


def body(weight):
    full = np.kron(sylvester(8), paley_signs())
    order = np.concatenate(
        [a * SUB + np.arange(r0, r0 + n) for r0, n in chunks() for a in range(4)]
    )
    left = jnp.asarray(full[order], jnp.bfloat16)
    right = jnp.asarray(sylvester(256), jnp.bfloat16)
    count = len(SIZES)
    f32, bf16 = jnp.float32, jnp.bfloat16
    rows_out = FF // N_G
    blocks = rows_out // BLOCK
    dma = pltpu.SemaphoreType.DMA
    mixed = pl.pallas_call(
        kernel,
        out_shape=pltpu.VMEM((rows_out, 128), f32),
        in_specs=[pl.BlockSpec(memory_space=pltpu.HBM)] * 3,
        out_specs=pl.BlockSpec(memory_space=pltpu.VMEM),
        scratch_shapes=[
            pltpu.VMEM((ROWS, COLS), bf16),
            pltpu.VMEM((ROWS, ROWS), bf16),
            pltpu.VMEM((256, 256), bf16),
            pltpu.VMEM((8, 4 * max(SIZES), 256), f32),
            *[pltpu.VMEM((N_F * SUB, 128), f32)] * 4,
            dma((3,)),
            *[dma((count,))] * 4,
        ],
        compiler_params=pltpu.CompilerParams(
            collective_id=0, has_side_effects=True, vmem_limit_bytes=60 << 20
        ),
        name="rotate",
    )(weight, left, right)
    quantized, scales = pl.pallas_call(
        finish,
        out_shape=(
            jax.ShapeDtypeStruct((rows_out, 128), bf16),
            jax.ShapeDtypeStruct((1, blocks), f32),
        ),
        in_specs=[pl.BlockSpec(memory_space=pltpu.VMEM)],
        out_specs=(
            pl.BlockSpec(memory_space=pltpu.HBM),
            pl.BlockSpec(memory_space=pltpu.VMEM),
        ),
        scratch_shapes=[
            pltpu.VMEM((rows_out, 128), bf16),
            pltpu.SemaphoreType.DMA((blocks // FINISH,)),
        ],
        compiler_params=pltpu.CompilerParams(vmem_limit_bytes=16 << 20),
        name="finish",
    )(mixed)
    return quantized, scales.reshape(blocks, 1)


def solution(mesh):
    in_specs = (P("fsdp", "grp"),)
    out_specs = (P("grp", "fsdp"), P("grp", "fsdp"))
    return jax.shard_map(body, mesh=mesh, in_specs=in_specs, out_specs=out_specs, check_vma=False)
```
